256 devices in a mesh: row: 8 (over x, core), col: 32 (over y, z).
Axes of the slice: x: 4, y: 4, z: 8, core: 2. Of those that a mesh axis runs over, the one named last changes fastest.
Arguments:
- factor: float32 [6, 8, 32, 512, 512], P(None, 'row', 'col'), may hold values from -0.1875 to 0.1875
- rhs: float32 [6, 8, 32, 128, 128], P(None, 'row', 'col'), may hold values from -6 to 6
- inverses: float32 [4, 512, 512], replicated, may hold values from -0.5 to 2, as said below
Outputs:
- solved: float32 [4, 512, 128], P(None, 'col')
- remaining: float32 [6, 8, 32, 128, 128], P(None, 'row', 'col')
The draws below stay inside these ranges and needn't reach their ends.
Inputs may be any that keep to these rules, and one draw needn't show every extreme that they name: `inverses`: each block is lower triangular with its diagonal between 0.5 and 2 and entries below it of magnitude at most 4 / sqrt(512).
All inputs are finite; a program needn't handle non-finite values.
Results may differ from the reference program's by a relative error of at most 0.00011.
Values sent between devices are 32-bit elements; how exact they have to be, the bound alone decides.
A program may use at most 64 MiB of HBM per device.

```python
import jax
import jax.numpy as jnp
from jax import lax

NB = 512
NRHS = 128
KSTEPS = 4
RB = 6
N_ROW = 8
N_COL = 32


def draw_inverses(key, part):
    first, second = jax.random.split(key)
    lower = jnp.clip(jax.random.normal(first, (KSTEPS, NB, NB), jnp.float32), -4.0, 4.0)
    diagonal = jax.random.uniform(second, (KSTEPS, NB), jnp.float32, 0.5, 2.0)
    row_pos = jnp.arange(NB)[:, None]
    col_pos = jnp.arange(NB)[None, :]
    below = (col_pos < row_pos).astype(jnp.float32)
    unit = (col_pos == row_pos).astype(jnp.float32)
    return lower * below * NB ** (-0.5) + unit * diagonal[:, :, None]


def block_levels(key, dims, cuts, least, largest):
    def one(dim, shards_of):
        draws = jax.random.uniform(jax.random.fold_in(jax.random.fold_in(key, 6), dim), (shards_of,), jnp.float32, least / len(cuts), largest / len(cuts))
        return jnp.repeat(jnp.exp(draws), dims[dim] // shards_of).reshape((-1,) + (1,) * (len(dims) - dim - 1))

    level = one(*cuts[0])
    for cut in cuts[1:]:
        level = level * one(*cut)
    return level


def centred(stream_key, extent, deviation, bound, shards=(), kind=jnp.bfloat16):
    result = deviation * jax.random.normal(stream_key, extent, jnp.float32)
    if shards:
        result = result * block_levels(stream_key, extent, shards, -0.22, 0.18)
    return jnp.clip(result, -bound, bound).astype(kind)


def setup_inputs(seed: int = 0) -> dict:
    streams_of = jax.random.split(jax.random.key(seed), 4)
    return {
        "factor": centred(streams_of[0], (RB, N_ROW, N_COL, NB, NB), (2 * NB) ** -0.5, 0.1875, ((1, 8), (2, 32)), jnp.float32),
        "rhs": centred(streams_of[1], (RB, N_ROW, N_COL, NB // KSTEPS, NRHS), 1.0, 6.0, ((1, 8), (2, 32)), jnp.float32),
        "inverses": draw_inverses(jax.random.fold_in(streams_of[3], 71), 0),
    }


def reference(factor, rhs, inverses):
    groups = N_COL // KSTEPS
    quarter = NB // KSTEPS
    block_ids = (jnp.arange(RB, dtype=jnp.int32)[:, None, None] * N_ROW + jnp.arange(N_ROW, dtype=jnp.int32)[None, :, None]) * groups + (jnp.arange(N_COL, dtype=jnp.int32) % groups)[None, None, :]
    current = rhs
    solved_list = []
    for k in range(KSTEPS):
        owner_row = k // groups
        owner_group = k % groups
        residual_block = current[0, owner_row, owner_group::groups].reshape(NB, NRHS)
        solved_block = jnp.dot(inverses[k], residual_block, precision=lax.Precision.HIGHEST)
        solved_list.append(solved_block)
        column_blocks = factor[:, :, k * groups:(k + 1) * groups]
        update = jnp.einsum("abgji,jh->abgih", column_blocks, solved_block, precision=lax.Precision.HIGHEST)
        update = update.reshape(RB, N_ROW, groups, KSTEPS, quarter, NRHS).transpose(0, 1, 3, 2, 4, 5).reshape(RB, N_ROW, N_COL, quarter, NRHS)
        keep = (block_ids > k).astype(jnp.float32)[:, :, :, None, None]
        current = current - update * keep
    return jnp.stack(solved_list), current
```

```python
import functools

import jax
import jax.numpy as jnp
from jax import lax
from jax.experimental import pallas as pl
from jax.experimental.pallas import tpu as pltpu
from jax.sharding import PartitionSpec as P

MESH = pl.DeviceIdType.MESH
F32 = jnp.float32
BF16 = jnp.bfloat16


def split(x):
    hi = x.astype(BF16)
    return hi, (x - hi.astype(F32)).astype(BF16)


def product(x, hi, lo, transposed=False):
    dims = (((1,), (1 if transposed else 0,)), ((), ()))
    m = x.shape[0]
    x_hi, x_lo = split(x)
    both = lax.dot_general(
        jnp.concatenate([x_hi, x_lo], axis=0), hi, dims, preferred_element_type=F32
    )
    return both[:m] + (both[m:] + lax.dot_general(x_hi, lo, dims, preferred_element_type=F32))


def assemble(tiles):
    blocks = tiles.reshape(4, 64, 128)
    return jnp.concatenate([blocks[b] for b in range(4)], axis=1)


def kernel(
    factor, rhs, inverses, solved_out, remaining_out,
    f32_buf, f_hi, f_lo, inv_f32, inv_hi, inv_lo, rhs_buf,
    first, own, direct, u_in, u_out, tiles, gathered, parts, received, turned, solved_in,
    f_sem, inv_sem, rhs_sem, self_sem,
    first_send, first_recv, own_send, own_recv, direct_send, direct_recv, u_send, u_recv,
    scatter_send, scatter_recv, gather_send, gather_recv, pair_send, pair_recv,
    part_send, part_recv, solved_send, solved_recv,
):
    row = lax.axis_index("row")
    col = lax.axis_index("col")
    y = col // 8
    z = lax.rem(col, 8)
    core = lax.rem(row, 2)
    x = row // 2
    chip = x * 8 + z
    blocks = f_hi.shape[0]

    on_chain = (row == 0) & (y < z) & (z <= 3)
    starts = on_chain & (y == 0)
    solves = on_chain & (z == y + 1)
    source = solves | ((row == 0) & (y == 0) & (z == 3))
    gives_first = (row == 0) & (z == 0)
    gives_own = (row == 0) & (z >= 1) & (z <= 3)

    def remote(src, dst, send, recv, to_row, to_col):
        return pltpu.make_async_remote_copy(
            src_ref=src, dst_ref=dst, send_sem=send, recv_sem=recv,
            device_id=(to_row, to_col), device_id_type=MESH,
        )

    def landed(ref, sem):
        remote(ref, ref, sem, sem, row, col).wait_recv()

    def left(ref, sem):
        remote(ref, ref, sem, sem, row, col).wait_send()

    barrier = pltpu.get_barrier_semaphore()

    def greet(to_row, to_col):
        pl.semaphore_signal(barrier, inc=1, device_id=(to_row, to_col), device_id_type=MESH)

    for d in range(1, 4):
        greet(row, lax.rem(col + 8 * d, 32))

    @pl.when(starts)
    def _():
        for p in range(4):
            greet(0, p * 8)

    @pl.when(on_chain & (y > 0))
    def _():
        greet(0, (y - 1) * 8 + y)

    source_col = jnp.where(y == 0, 3, (y - 1) * 8 + y)

    @pl.when(jnp.logical_not((row == 0) & (col == source_col)))
    def _():
        greet(0, source_col)

    def f_load(a):
        return pltpu.make_async_copy(factor.at[a, 0, 0], f32_buf.at[a], f_sem.at[a])

    def inv_load(k, slot):
        return pltpu.make_async_copy(inverses.at[k], inv_f32.at[slot], inv_sem.at[slot])

    @pl.when(starts)
    def _():
        inv_load(0, 0).start()

    @pl.when(solves)
    def _():
        inv_load(z, 1).start()

    for a in range(blocks):
        f_load(a).start()
    rhs_load = pltpu.make_async_copy(rhs.at[:, 0, 0], rhs_buf, rhs_sem)
    rhs_load.start()
    self_load = pltpu.make_async_copy(rhs.at[0, 0, 0], own.at[y], self_sem)

    @pl.when(solves)
    def _():
        self_load.start()

    def split_inverse(k, slot):
        inv_load(k, slot).wait()
        hi, lo = split(inv_f32[slot])
        inv_hi[slot] = hi
        inv_lo[slot] = lo

    def split_factor(a):
        f_load(a).wait()
        hi, lo = split(f32_buf[a])
        f_hi[a] = hi
        f_lo[a] = lo

    @pl.when(starts)
    def _():
        split_inverse(0, 0)

    @pl.when(solves)
    def _():
        split_inverse(z, 1)

    split_factor(0)

    greeted = 3
    greeted += jnp.where(gives_first, 3, 0)
    greeted += jnp.where(source, jnp.where((y == 0) & (z == 3), 63, 64), 0)
    greeted += jnp.where(solves & (z < 3), 3 - z, 0)
    pl.semaphore_wait(barrier, greeted)

    @pl.when(gives_first)
    def _():
        for t in range(1, 4):
            remote(rhs.at[0, 0, 0], first.at[y], first_send, first_recv.at[y], 0, t).start()

    @pl.when(gives_own & (y != z - 1))
    def _():
        remote(rhs.at[0, 0, 0], own.at[y], own_send, own_recv.at[y], 0, (z - 1) * 8 + z).start()

    def split_rest():
        lax.fori_loop(1, blocks, lambda a, _: (split_factor(a), 0)[1], 0)

    @pl.when(jnp.logical_not(starts))
    def _():
        split_rest()

    def store_tiles(s):
        for c in range(2):
            for b in range(4):
                tiles[c, b * 8 : (b + 1) * 8] = s[
                    64 * c : 64 * (c + 1), 128 * b : 128 * (b + 1)
                ].reshape(8, 8, 128)

    def scatter(plane):
        def send(i, _):
            to_row = i // 8
            to_z = lax.rem(i, 8)
            here = (to_row == row) & (plane * 8 + to_z == col)
            piece = (lax.rem(to_row, 2), (to_row // 2) * 8 + to_z)

            @pl.when(jnp.logical_not(here))
            def _():
                remote(
                    tiles.at[piece], gathered.at[piece], scatter_send, scatter_recv,
                    to_row, plane * 8 + to_z,
                ).start()

            return 0

        lax.fori_loop(0, 64, send, 0)

    @pl.when(on_chain)
    def _():
        @pl.when(y == 0)
        def _():
            for p in range(4):
                landed(first.at[p], first_recv.at[p])
            v = jnp.concatenate([first[p].T for p in range(4)], axis=1)
            s = product(v, inv_hi[0], inv_lo[0], True)
            direct_value = s
            for c in range(2):
                for b in range(4):
                    direct[c, b * 8 : (b + 1) * 8] = direct_value[
                        64 * c : 64 * (c + 1), 128 * b : 128 * (b + 1)
                    ].reshape(8, 8, 128)

        @pl.when(y > 0)
        def _():
            landed(direct, direct_recv)

        s = jnp.concatenate([assemble(direct[0]), assemble(direct[1])], axis=0)
        u_out[...] = product(s, f_hi[0], f_lo[0])

        @pl.when(z > y + 1)
        def _():
            remote(u_out, u_in.at[y], u_send, u_recv.at[y], 0, (z - 1) * 8 + z).start()

        @pl.when((y == 0) & (z == 3))
        def _():
            tiles[...] = direct[...]
            gathered[core, chip] = direct[core, chip]
            scatter(0)

        @pl.when(z == y + 1)
        def _():
            self_load.wait()
            for p in range(4):

                @pl.when(p != y)
                def _(p=p):
                    landed(own.at[p], own_recv.at[p])

            for j in range(2):

                @pl.when(j < y)
                def _(j=j):
                    landed(u_in.at[j], u_recv.at[j])
                    u_out[...] += u_in[j]

            v = jnp.concatenate([own[p].T for p in range(4)], axis=1) - u_out[...]
            store_tiles(product(v, inv_hi[1], inv_lo[1], True))
            for t in range(2, 4):

                @pl.when(t > z)
                def _(t=t):
                    remote(tiles, direct, direct_send.at[t - 2], direct_recv, 0, z * 8 + t).start()

            scatter(z)

        @pl.when(y == 0)
        def _():
            split_rest()

    @pl.when(jnp.logical_not((row == 0) & (col == 3)))
    def _():
        landed(gathered.at[core, chip], scatter_recv)

    mine = gathered.at[core, chip]

    def send_tile(i, _):
        to_row = lax.rem(x + i // 8, 4) * 2 + core
        to_col = y * 8 + lax.rem(z + lax.rem(i, 8), 8)
        remote(mine, mine, gather_send, gather_recv, to_row, to_col).start()
        return 0

    lax.fori_loop(1, 32, send_tile, 0)
    landed(gathered.at[core, pl.ds(0, 31)], gather_recv)
    other = row + 1 - 2 * core
    pair = remote(gathered.at[core], gathered.at[core], pair_send, pair_recv, other, col)
    pair.start()

    keep = jnp.where((row == 0) & (z <= y), 0.0, 1.0).astype(F32)

    def update(half):
        s = assemble(gathered[half])

        def one(a, _):
            u = product(s, f_hi[a], f_lo[a])
            u = jnp.where(a == 0, u * keep, u)
            for p in range(4):
                parts[p, half, a] = u[:, 128 * p : 128 * (p + 1)]

            received[y, half, a] = parts[y, half, a]
            for d in range(1, 4):
                to = lax.rem(y + d, 4)
                remote(
                    parts.at[to, half, a], received.at[y, half, a], part_send, part_recv.at[y, half],
                    row, to * 8 + z,
                ).start()
            return 0

        lax.fori_loop(0, blocks, one, 0)

    update(core)
    landed(gathered.at[1 - core], pair_recv)
    update(1 - core)

    for b in range(4):
        t = jnp.concatenate(
            [gathered[0, b * 8 : (b + 1) * 8], gathered[1, b * 8 : (b + 1) * 8]], axis=0
        ).reshape(128, 128)
        turned[b] = t.T
    rows = pl.ds(pl.multiple_of(z * 16, 16), 16)
    for d in range(1, 4):
        to = lax.rem(y + d, 4)
        remote(
            turned.at[to, rows], solved_in.at[y], solved_send, solved_recv.at[y], row, to * 8 + z
        ).start()
    solved_in[y] = turned[y, rows]

    rhs_load.wait()

    def reduce(k):
        def one(a, _):
            part = jnp.concatenate([received[k, 0, a], received[k, 1, a]], axis=0)
            rhs_buf[a] = rhs_buf[a] - part.T
            return 0

        lax.fori_loop(0, blocks, one, 0)

    for k in range(4):

        @pl.when(k != y)
        def _(k=k):
            landed(received.at[k, 0], part_recv.at[k, 0])
            landed(received.at[k, 1], part_recv.at[k, 1])

        reduce(k)
    remaining_out[...] = rhs_buf[...]
    for k in range(4):

        @pl.when(k != y)
        def _(k=k):
            landed(solved_in.at[k], solved_recv.at[k])

    solved_out[...] = solved_in[...]

    left(solved_in.at[pl.ds(0, 3)], solved_send)
    left(received.at[pl.ds(0, 3)], part_send)
    pair.wait_send()
    left(gathered.at[core, pl.ds(0, 31)], gather_send)

    @pl.when(gives_first)
    def _():
        left(first.at[pl.ds(0, 3)], first_send)

    @pl.when(gives_own & (y != z - 1))
    def _():
        left(own.at[0], own_send)

    @pl.when(on_chain & (z > y + 1))
    def _():
        left(u_out, u_send)

    @pl.when(solves)
    def _():
        for t in range(2, 4):

            @pl.when(t > z)
            def _(t=t):
                left(tiles, direct_send.at[t - 2])

        left(tiles, scatter_send)

    @pl.when((row == 0) & (col == 3))
    def _():
        left(tiles.at[0], scatter_send)
        left(tiles.at[1, pl.ds(0, 31)], scatter_send)


def solution(mesh):
    def on_device(factor, rhs, inverses):
        steps = inverses.shape[0]
        blocks, width, nrhs = factor.shape[0], factor.shape[3], rhs.shape[4]
        vmem, dma = pltpu.VMEM, pltpu.SemaphoreType.DMA
        solved, remaining = pl.pallas_call(
            kernel,
            out_shape=(
                jax.ShapeDtypeStruct((steps, 16, nrhs), F32),
                jax.ShapeDtypeStruct((blocks, 128, nrhs), F32),
            ),
            in_specs=[pl.BlockSpec(memory_space=pl.ANY)] * 3,
            out_specs=(
                pl.BlockSpec(memory_space=pltpu.VMEM),
                pl.BlockSpec(memory_space=pltpu.VMEM),
            ),
            scratch_shapes=[
                vmem((blocks, width, width), F32),
                vmem((blocks, width, width), BF16),
                vmem((blocks, width, width), BF16),
                vmem((2, width, width), F32),
                vmem((2, width, width), BF16),
                vmem((2, width, width), BF16),
                vmem((blocks, 128, nrhs), F32),
                vmem((4, 128, nrhs), F32),
                vmem((4, 128, nrhs), F32),
                vmem((2, 32, 8, 128), F32),
                vmem((2, nrhs, width), F32),
                vmem((nrhs, width), F32),
                vmem((2, 32, 8, 128), F32),
                vmem((2, 32, 8, 128), F32),
                vmem((4, 2, blocks, 64, 128), F32),
                vmem((4, 2, blocks, 64, 128), F32),
                vmem((4, 128, nrhs), F32),
                vmem((4, 16, nrhs), F32),
                dma((blocks,)),
                dma((2,)),
                dma,
                dma,
                dma,
                dma((4,)),
                dma,
                dma((4,)),
                dma((2,)),
                dma,
                dma,
                dma((2,)),
                dma,
                dma,
                dma,
                dma,
                dma,
                dma,
                dma,
                dma((4, 2)),
                dma,
                dma((4,)),
            ],
            compiler_params=pltpu.CompilerParams(
                collective_id=0, has_side_effects=True, vmem_limit_bytes=56 * 2**20
            ),
        )(factor, rhs, inverses)
        return solved, remaining[:, None, None]

    return jax.shard_map(
        on_device,
        mesh=mesh,
        in_specs=(P(None, "row", "col", None, None), P(None, "row", "col", None, None), P()),
        out_specs=(P(None, "col", None), P(None, "row", "col", None, None)),
        check_vma=False,
    )
```

```python
import jax
import jax.numpy as jnp
from jax import lax
from jax.experimental import pallas as pl
from jax.experimental.pallas import tpu as pltpu
from jax.sharding import PartitionSpec as P

MESH = pl.DeviceIdType.MESH
F32 = jnp.float32
BF16 = jnp.bfloat16


def split(x):
    hi = x.astype(BF16)
    return hi, (x - hi.astype(F32)).astype(BF16)


def product(x, hi, lo, transposed=False):
    dims = (((1,), (1 if transposed else 0,)), ((), ()))
    m = x.shape[0]
    x_hi, x_lo = split(x)
    both = lax.dot_general(
        jnp.concatenate([x_hi, x_lo], axis=0), hi, dims, preferred_element_type=F32
    )
    return both[:m] + (both[m:] + lax.dot_general(x_hi, lo, dims, preferred_element_type=F32))


def kernel(
    factor, rhs, inverses, solved_out, remaining_out,
    f32_buf, f_hi, f_lo, inv_f32, inv_hi, inv_lo, rhs_buf, total,
    first, own, first_t, own_t, direct, u_in, u_out, s_out, gathered,
    parts, received, turned, solved_in,
    f_sem, inv_sem, rhs_sem, self_sem,
    first_send, first_recv, own_send, own_recv, direct_send, direct_recv, u_send, u_recv,
    plane_send, relay_send, plane_recv, part_send, part_recv, solved_send, solved_recv,
):
    row = lax.axis_index("row")
    col = lax.axis_index("col")
    y = col // 8
    z = lax.rem(col, 8)
    blocks = f_hi.shape[0]
    chunks, high = gathered.shape[0], gathered.shape[1]

    on_chain = (row == 0) & (y < z) & (z <= 3)
    starts = on_chain & (y == 0)
    solves = on_chain & (z == y + 1)
    opens = (row == 4) & (col == 0)
    gives_first = (row == 0) & (z == 0)
    gives_own = (row == 0) & (z >= 1) & (z <= 3)
    relay_row = jnp.where(y == 0, 4, 0)
    relays = row == relay_row

    def remote(src, dst, send, recv, to_row, to_col):
        return pltpu.make_async_remote_copy(
            src_ref=src, dst_ref=dst, send_sem=send, recv_sem=recv,
            device_id=(to_row, to_col), device_id_type=MESH,
        )

    def landed(ref, sem):
        remote(ref, ref, sem, sem, row, col).wait_recv()

    def left(ref, sem):
        remote(ref, ref, sem, sem, row, col).wait_send()

    def each(n, body):
        lax.fori_loop(0, n, lambda i, _: (body(i), 0)[1], 0)

    barrier = pltpu.get_barrier_semaphore()

    def greet(to_row, to_col):
        pl.semaphore_signal(barrier, inc=1, device_id=(to_row, to_col), device_id_type=MESH)

    @pl.when(starts | opens)
    def _():
        for p in range(4):
            greet(0, p * 8)

    for d in range(1, 4):
        greet(row, lax.rem(col + 8 * d, 32))

    @pl.when(relays & jnp.logical_not(opens))
    def _():
        greet(relay_row, jnp.where(y == 0, 0, (y - 1) * 8 + y))

    @pl.when(jnp.logical_not(relays))
    def _():
        greet(relay_row, col)

    def f_load(a):
        return pltpu.make_async_copy(factor.at[a, 0, 0], f32_buf.at[a], f_sem.at[a])

    def inv_load(k, slot):
        return pltpu.make_async_copy(inverses.at[k], inv_f32.at[slot], inv_sem.at[slot])

    @pl.when(starts | opens)
    def _():
        inv_load(0, 0).start()

    @pl.when(solves)
    def _():
        inv_load(z, 1).start()

    for a in range(blocks):
        f_load(a).start()
    rhs_load = pltpu.make_async_copy(rhs.at[:, 0, 0], rhs_buf, rhs_sem)
    rhs_load.start()
    self_load = pltpu.make_async_copy(rhs.at[0, 0, 0], own.at[y], self_sem)

    @pl.when(solves)
    def _():
        self_load.start()

    def split_inverse(k, slot):
        inv_load(k, slot).wait()
        hi, lo = split(inv_f32[slot])
        inv_hi[slot] = hi
        inv_lo[slot] = lo

    def split_factor(a):
        f_load(a).wait()
        hi, lo = split(f32_buf[a])
        f_hi[a] = hi
        f_lo[a] = lo

    @pl.when(starts | opens)
    def _():
        split_inverse(0, 0)

    @pl.when(solves)
    def _():
        split_inverse(z, 1)

    split_factor(0)

    greeted = 3
    greeted += jnp.where(gives_first, 4, 0)
    greeted += jnp.where(solves, 8, 0)
    greeted += jnp.where(opens, 7, 0)
    greeted += jnp.where(relays, 7, 0)
    pl.semaphore_wait(barrier, greeted)

    @pl.when(gives_first)
    def _():
        for t in range(1, 4):
            remote(rhs.at[0, 0, 0], first.at[y], first_send, first_recv.at[y], 0, t).start()
        remote(rhs.at[0, 0, 0], first.at[y], first_send, first_recv.at[y], 4, 0).start()

    @pl.when(gives_own & (y != z - 1))
    def _():
        remote(rhs.at[0, 0, 0], own.at[y], own_send, own_recv.at[y], 0, (z - 1) * 8 + z).start()

    def prepare():
        lax.fori_loop(1, blocks, lambda a, _: (split_factor(a), 0)[1], 0)
        rhs_load.wait()

        def turn(a):
            total[a] = rhs_buf[a].T

        each(blocks, turn)

    early = starts | opens

    @pl.when(jnp.logical_not(early))
    def _():
        prepare()

    def rows_of(q):
        return pl.ds(pl.multiple_of(q * high, high), high)

    def spread(q, plane):
        for t in range(8):
            remote(
                s_out.at[q], gathered.at[q], plane_send, plane_recv.at[q], 0, plane * 8 + t
            ).start()

    @pl.when(early)
    def _():
        for p in range(4):
            landed(first.at[p], first_recv.at[p])
            first_t[:, 128 * p : 128 * (p + 1)] = first[p].T

    @pl.when(opens)
    def _():
        def open_chunk(q):
            gathered[q] = product(first_t[rows_of(q)], inv_hi[0], inv_lo[0], True)
            for t in range(1, 8):
                remote(
                    gathered.at[q], gathered.at[q], plane_send, plane_recv.at[q], 4, t
                ).start()

        each(chunks, open_chunk)

    @pl.when(on_chain)
    def _():
        @pl.when(z == y + 1)
        def _():
            self_load.wait()
            for p in range(4):

                @pl.when(p != y)
                def _(p=p):
                    landed(own.at[p], own_recv.at[p])

                own_t[:, 128 * p : 128 * (p + 1)] = own[p].T

        def chain_chunk(q):
            @pl.when(y == 0)
            def _():
                direct[q] = product(first_t[rows_of(q)], inv_hi[0], inv_lo[0], True)

            @pl.when(y > 0)
            def _():
                landed(direct.at[q], direct_recv.at[q])

            u = product(direct[q], f_hi[0], f_lo[0])

            @pl.when(z > y + 1)
            def _():
                u_out[q] = u
                remote(
                    u_out.at[q], u_in.at[y, q], u_send, u_recv.at[y, q], 0, (z - 1) * 8 + z
                ).start()

            @pl.when(z == y + 1)
            def _():
                u_out[q] = own_t[rows_of(q)] - u
                for j in range(2):

                    @pl.when(j < y)
                    def _(j=j):
                        landed(u_in.at[j, q], u_recv.at[j, q])
                        u_out[q] = u_out[q] - u_in[j, q]

                s_out[q] = product(u_out[q], inv_hi[1], inv_lo[1], True)
                for t in range(2, 4):

                    @pl.when(t > z)
                    def _(t=t):
                        remote(
                            s_out.at[q], direct.at[q], direct_send, direct_recv.at[q], 0, z * 8 + t
                        ).start()

                @pl.when(z == 3)
                def _():
                    spread(q, 3)

        each(chunks, chain_chunk)

        @pl.when((z == y + 1) & (z < 3))
        def _():
            each(chunks, lambda q: spread(q, z))

    @pl.when(early)
    def _():
        prepare()

    keep = jnp.where((row == 0) & (z <= y), 0.0, 1.0).astype(F32)

    def plane_chunk(q):
        @pl.when(jnp.logical_not(opens))
        def _():
            landed(gathered.at[q], plane_recv.at[q])

        @pl.when(relays)
        def _():
            for t in range(1, 8):
                remote(
                    gathered.at[q], gathered.at[q], relay_send, plane_recv.at[q],
                    lax.rem(row + t, 8), col,
                ).start()

        s = gathered[q]

        def one(a):
            u = product(s, f_hi[a], f_lo[a])
            u = jnp.where(a == 0, u * keep, u)
            for p in range(4):
                parts[p, q, a] = u[:, 128 * p : 128 * (p + 1)]

            received[y, q, a] = parts[y, q, a]
            for d in range(1, 4):
                to = lax.rem(y + d, 4)
                remote(
                    parts.at[to, q, a], received.at[y, q, a], part_send, part_recv.at[y, q],
                    row, to * 8 + z,
                ).start()

        each(blocks, one)

    each(chunks, plane_chunk)

    for b in range(4):
        t = jnp.concatenate(
            [gathered[q, :, 128 * b : 128 * (b + 1)] for q in range(chunks)], axis=0
        )
        turned[b] = t.T
    rows = pl.ds(pl.multiple_of(z * 16, 16), 16)
    for d in range(1, 4):
        to = lax.rem(y + d, 4)
        remote(
            turned.at[to, rows], solved_in.at[y], solved_send, solved_recv.at[y], row, to * 8 + z
        ).start()
    solved_in[y] = turned[y, rows]

    for k in range(4):

        def reduce(q, k=k):
            @pl.when(k != y)
            def _():
                landed(received.at[k, q], part_recv.at[k, q])

            def one(a):
                total[a, rows_of(q)] = total[a, rows_of(q)] - received[k, q, a]

            each(blocks, one)

        each(chunks, reduce)

    for a in range(blocks):
        remaining_out[a] = total[a].T
    for k in range(4):

        @pl.when(k != y)
        def _(k=k):
            landed(solved_in.at[k], solved_recv.at[k])

    solved_out[...] = solved_in[...]

    left(solved_in.at[pl.ds(0, 3)], solved_send)
    left(received.at[pl.ds(0, 3)], part_send)

    @pl.when(relays)
    def _():
        for t in range(1, 8):
            left(gathered, relay_send)

    @pl.when(gives_first)
    def _():
        left(first, first_send)

    @pl.when(gives_own & (y != z - 1))
    def _():
        left(own.at[0], own_send)

    @pl.when(on_chain & (z > y + 1))
    def _():
        left(u_out, u_send)

    @pl.when(solves)
    def _():
        for t in range(2, 4):

            @pl.when(t > z)
            def _(t=t):
                left(s_out, direct_send)

        for t in range(8):
            left(s_out, plane_send)

    @pl.when(opens)
    def _():
        for t in range(1, 8):
            left(gathered, plane_send)


def write(solved, remaining, solved_out, remaining_out, sems):
    copies = [
        pltpu.make_async_copy(remaining, remaining_out, sems.at[0]),
        pltpu.make_async_copy(solved, solved_out, sems.at[1]),
    ]
    for c in copies:
        c.start()
    for c in copies:
        c.wait()


def solution(mesh):
    def on_device(factor, rhs, inverses):
        steps = inverses.shape[0]
        blocks, width, nrhs = factor.shape[0], factor.shape[3], rhs.shape[4]
        chunks = 4
        high = nrhs // chunks
        vmem, dma = pltpu.VMEM, pltpu.SemaphoreType.DMA
        shapes = (
            jax.ShapeDtypeStruct((steps, 16, nrhs), F32),
            jax.ShapeDtypeStruct((blocks, 128, nrhs), F32),
        )
        results = pl.pallas_call(
            kernel,
            out_shape=shapes,
            in_specs=[pl.BlockSpec(memory_space=pl.ANY)] * 3,
            out_specs=(pl.BlockSpec(memory_space=pltpu.VMEM),) * 2,
            scratch_shapes=[
                vmem((blocks, width, width), F32),
                vmem((blocks, width, width), BF16),
                vmem((blocks, width, width), BF16),
                vmem((2, width, width), F32),
                vmem((2, width, width), BF16),
                vmem((2, width, width), BF16),
                vmem((blocks, 128, nrhs), F32),
                vmem((blocks, nrhs, 128), F32),
                vmem((4, 128, nrhs), F32),
                vmem((4, 128, nrhs), F32),
                vmem((nrhs, width), F32),
                vmem((nrhs, width), F32),
                vmem((chunks, high, width), F32),
                vmem((2, chunks, high, width), F32),
                vmem((chunks, high, width), F32),
                vmem((chunks, high, width), F32),
                vmem((chunks, high, width), F32),
                vmem((4, chunks, blocks, high, 128), F32),
                vmem((4, chunks, blocks, high, 128), F32),
                vmem((4, 128, nrhs), F32),
                vmem((4, 16, nrhs), F32),
                dma((blocks,)),
                dma((2,)),
                dma,
                dma,
                dma,
                dma((4,)),
                dma,
                dma((4,)),
                dma,
                dma((chunks,)),
                dma,
                dma((2, chunks)),
                dma,
                dma,
                dma((chunks,)),
                dma,
                dma((4, chunks)),
                dma,
                dma((4,)),
            ],
            compiler_params=pltpu.CompilerParams(
                collective_id=0, has_side_effects=True, vmem_limit_bytes=56 * 2**20
            ),
        )(factor, rhs, inverses)
        solved, remaining = pl.pallas_call(
            write,
            out_shape=shapes,
            in_specs=[pl.BlockSpec(memory_space=pl.ANY)] * 2,
            out_specs=(pl.BlockSpec(memory_space=pl.ANY),) * 2,
            scratch_shapes=[dma((2,))],
        )(*results)
        return solved, remaining[:, None, None]

    return jax.shard_map(
        on_device,
        mesh=mesh,
        in_specs=(P(None, "row", "col", None, None), P(None, "row", "col", None, None), P()),
        out_specs=(P(None, "col", None), P(None, "row", "col", None, None)),
        check_vma=False,
    )
```

```python
import jax
import jax.numpy as jnp
from jax import lax
from jax.experimental import pallas as pl
from jax.experimental.pallas import tpu as pltpu
from jax.sharding import PartitionSpec as P

MESH = pl.DeviceIdType.MESH
F32 = jnp.float32
BF16 = jnp.bfloat16
SIZES = (24, 24, 24, 24, 16, 16)
CHUNKS = tuple((sum(SIZES[:q]), n) for q, n in enumerate(SIZES))


def split(x):
    hi = x.astype(BF16)
    return hi, (x - hi.astype(F32)).astype(BF16)


def product(x, hi, lo, transposed=False):
    dims = (((1,), (1 if transposed else 0,)), ((), ()))
    m = x.shape[0]
    x_hi, x_lo = split(x)
    both = lax.dot_general(
        jnp.concatenate([x_hi, x_lo], axis=0), hi, dims, preferred_element_type=F32
    )
    return both[:m] + (both[m:] + lax.dot_general(x_hi, lo, dims, preferred_element_type=F32))


def kernel(
    factor, rhs, inverses, solved_out, remaining_out,
    f32_buf, f_hi, f_lo, inv_f32, inv_hi, inv_lo, m_f32, m_hi, m_lo, rhs_buf, total,
    first, own, first_t, own_t, direct, u_in, u_out, s_out, gathered,
    parts, received, turned, solved_in,
    f_sem, inv_sem, rhs_sem, self_sem,
    first_send, first_recv, own_send, own_recv, direct_send, direct_recv, u_send, u_recv,
    plane_send, relay_send, plane_recv, part_send, part_recv, solved_send, solved_recv,
):
    row = lax.axis_index("row")
    col = lax.axis_index("col")
    y = col // 8
    z = lax.rem(col, 8)
    blocks = f_hi.shape[0]

    on_chain = (row == 0) & (y < z) & (z <= 3)
    starts = on_chain & (y == 0)
    solves = on_chain & (z == y + 1)
    opens = (row == 4) & (col == 0)
    gives_first = (row == 0) & (z == 0)
    gives_own = (row == 0) & (z >= 1) & (z <= 3)
    relay_row = jnp.where(y == 0, 5, 1)
    relays = row == relay_row

    def remote(src, dst, send, recv, to_row, to_col):
        return pltpu.make_async_remote_copy(
            src_ref=src, dst_ref=dst, send_sem=send, recv_sem=recv,
            device_id=(to_row, to_col), device_id_type=MESH,
        )

    def landed(ref, sem):
        remote(ref, ref, sem, sem, row, col).wait_recv()

    def left(ref, sem):
        remote(ref, ref, sem, sem, row, col).wait_send()

    def each(n, body):
        lax.fori_loop(0, n, lambda i, _: (body(i), 0)[1], 0)

    barrier = pltpu.get_barrier_semaphore()

    def greet(to_row, to_col):
        pl.semaphore_signal(barrier, inc=1, device_id=(to_row, to_col), device_id_type=MESH)

    @pl.when(starts | opens)
    def _():
        for p in range(4):
            greet(0, p * 8)

    for d in range(1, 4):
        greet(row, lax.rem(col + 8 * d, 32))

    @pl.when(relays)
    def _():
        greet(jnp.where(y == 0, 4, 0), jnp.where(y == 0, 0, (y - 1) * 8 + y))

    @pl.when(on_chain & (y > 0))
    def _():
        greet(0, (y - 1) * 8 + y)

    @pl.when(jnp.logical_not(relays))
    def _():
        greet(relay_row, col)

    def f_load(a):
        return pltpu.make_async_copy(factor.at[a, 0, 0], f32_buf.at[a], f_sem.at[a])

    def inv_load(k, slot):
        return pltpu.make_async_copy(inverses.at[k], inv_f32.at[slot], inv_sem.at[slot])

    @pl.when(starts | opens)
    def _():
        inv_load(0, 0).start()

    @pl.when(on_chain)
    def _():
        inv_load(z, 1).start()

    for a in range(blocks):
        f_load(a).start()
    rhs_load = pltpu.make_async_copy(rhs.at[:, 0, 0], rhs_buf, rhs_sem)
    rhs_load.start()
    self_load = pltpu.make_async_copy(rhs.at[0, 0, 0], own.at[y], self_sem)

    @pl.when(solves)
    def _():
        self_load.start()

    def split_inverse(k, slot):
        inv_load(k, slot).wait()
        hi, lo = split(inv_f32[slot])
        inv_hi[slot] = hi
        inv_lo[slot] = lo

    def split_factor(a):
        f_load(a).wait()
        hi, lo = split(f32_buf[a])
        f_hi[a] = hi
        f_lo[a] = lo

    @pl.when(starts | opens)
    def _():
        split_inverse(0, 0)

    split_factor(0)

    def fold(source):
        def some(b):
            rows = pl.ds(pl.multiple_of(b * 128, 128), 128)
            m_f32[rows] = source(rows)

        each(4, some)

    def split_m():
        hi, lo = split(m_f32[...])
        m_hi[...] = hi
        m_lo[...] = lo

    @pl.when(on_chain)
    def _():
        split_inverse(z, 1)
        fold(lambda rows: product(f32_buf[0, rows], inv_hi[1], inv_lo[1], True))
        split_m()

        @pl.when(y == 0)
        def _():
            for b in range(4):
                for c in range(4):
                    f32_buf[0, 128 * b : 128 * (b + 1), 128 * c : 128 * (c + 1)] = inv_f32[
                        0, 128 * c : 128 * (c + 1), 128 * b : 128 * (b + 1)
                    ].T
            fold(lambda rows: product(f32_buf[0, rows], m_hi[...], m_lo[...]))
            split_m()

    greeted = 3
    greeted += jnp.where(gives_first, 4, 0)
    greeted += jnp.where(solves | opens, 8, 0)
    greeted += jnp.where(solves & (z < 3), 3 - z, 0)
    greeted += jnp.where(relays, 7, 0)
    pl.semaphore_wait(barrier, greeted)

    @pl.when(gives_first)
    def _():
        for t in range(1, 4):
            remote(rhs.at[0, 0, 0], first.at[y], first_send, first_recv.at[y], 0, t).start()
        remote(rhs.at[0, 0, 0], first.at[y], first_send, first_recv.at[y], 4, 0).start()

    @pl.when(gives_own & (y != z - 1))
    def _():
        remote(rhs.at[0, 0, 0], own.at[y], own_send, own_recv.at[y], 0, (z - 1) * 8 + z).start()

    def prepare():
        lax.fori_loop(1, blocks, lambda a, _: (split_factor(a), 0)[1], 0)
        rhs_load.wait()

        def turn(a):
            total[a] = rhs_buf[a].T

        each(blocks, turn)

    early = starts | opens

    @pl.when(jnp.logical_not(early))
    def _():
        prepare()

    def rows_of(q):
        return pl.ds(*CHUNKS[q])

    def each_chunk(body):
        for q in range(len(CHUNKS)):
            body(q)

    def spread(q, plane):
        relay_to = jnp.where(opens, 5, 1)
        for d in (4, 3, 5, 2, 6, 1, 7, 0):
            remote(
                s_out.at[rows_of(q)], gathered.at[rows_of(q)], plane_send, plane_recv.at[q],
                relay_to, plane * 8 + lax.rem(z + d, 8),
            ).start()

    @pl.when(solves)
    def _():
        self_load.wait()
        for p in range(4):

            @pl.when(p != y)
            def _(p=p):
                landed(own.at[p], own_recv.at[p])

            own_t[:, 128 * p : 128 * (p + 1)] = own[p].T

        own_t[...] = product(own_t[...], inv_hi[1], inv_lo[1], True)

    @pl.when(early)
    def _():
        for p in (0, 1, 3, 2):
            landed(first.at[p], first_recv.at[p])
            first_t[:, 128 * p : 128 * (p + 1)] = first[p].T

    @pl.when(opens)
    def _():
        def open_chunk(q):
            s_out[rows_of(q)] = product(first_t[rows_of(q)], inv_hi[0], inv_lo[0], True)
            spread(q, 0)

        each_chunk(open_chunk)

    @pl.when(on_chain)
    def _():
        def chain_chunk(q):
            rows = rows_of(q)

            @pl.when(y == 0)
            def _():
                direct[rows] = first_t[rows]

            @pl.when(y > 0)
            def _():
                landed(direct.at[rows], direct_recv.at[q])

            u = product(direct[rows], m_hi[...], m_lo[...])

            @pl.when(z > y + 1)
            def _():
                u_out[rows] = u
                remote(
                    u_out.at[rows], u_in.at[y, rows], u_send, u_recv.at[y, q], 0, (z - 1) * 8 + z
                ).start()

            @pl.when(z == y + 1)
            def _():
                s_out[rows] = own_t[rows] - u
                for j in range(2):

                    @pl.when(j < y)
                    def _(j=j):
                        landed(u_in.at[j, rows], u_recv.at[j, q])
                        s_out[rows] = s_out[rows] - u_in[j, rows]

                for t in range(2, 4):

                    @pl.when(t > z)
                    def _(t=t):
                        remote(
                            s_out.at[rows], direct.at[rows], direct_send, direct_recv.at[q],
                            0, z * 8 + t,
                        ).start()

                @pl.when(z >= 2)
                def _():
                    spread(q, z)

        each_chunk(chain_chunk)

        @pl.when((y == 0) & (z == 1))
        def _():
            each_chunk(lambda q: spread(q, z))

    @pl.when(early)
    def _():
        prepare()

    keep = jnp.where((row == 0) & (z <= y), 0.0, 1.0).astype(F32)

    def plane_chunk(q):
        rows = rows_of(q)

        landed(gathered.at[rows], plane_recv.at[q])

        @pl.when(relays)
        def _():
            for d in (3, 5, 4, 6, 1, 2, 7):
                remote(
                    gathered.at[rows], gathered.at[rows], relay_send, plane_recv.at[q],
                    lax.rem(row + d, 8), col,
                ).start()

        s = gathered[rows]

        def one(a):
            u = product(s, f_hi[a], f_lo[a])
            u = jnp.where(a == 0, u * keep, u)
            for p in range(4):
                parts[p, a, rows] = u[:, 128 * p : 128 * (p + 1)]

            received[y, a, rows] = parts[y, a, rows]
            for i in range(3):
                to = lax.rem(y + 1 + lax.rem(i + 1 - lax.rem(y, 2), 3), 4)
                remote(
                    parts.at[to, a, rows], received.at[y, a, rows], part_send, part_recv.at[y, q],
                    row, to * 8 + z,
                ).start()

        each(blocks, one)

    each_chunk(plane_chunk)

    for b in range(4):
        turned[b] = gathered[:, 128 * b : 128 * (b + 1)].T
    rows = pl.ds(pl.multiple_of(z * 16, 16), 16)
    for d in range(1, 4):
        to = lax.rem(y + d, 4)
        remote(
            turned.at[to, rows], solved_in.at[y], solved_send, solved_recv.at[y], row, to * 8 + z
        ).start()
    solved_in[y] = turned[y, rows]

    for k in range(4):

        def reduce(q, k=k):
            @pl.when(k != y)
            def _():
                landed(received.at[k, :, rows_of(q)], part_recv.at[k, q])

            def one(a):
                total[a, rows_of(q)] = total[a, rows_of(q)] - received[k, a, rows_of(q)]

            each(blocks, one)

        each_chunk(reduce)

    for a in range(blocks):
        remaining_out[a] = total[a].T
    for k in range(4):

        @pl.when(k != y)
        def _(k=k):
            landed(solved_in.at[k], solved_recv.at[k])

    solved_out[...] = solved_in[...]

    left(solved_in.at[pl.ds(0, 3)], solved_send)
    left(received.at[pl.ds(0, 3)], part_send)

    @pl.when(relays)
    def _():
        for t in range(1, 8):
            left(gathered, relay_send)

    @pl.when(gives_first)
    def _():
        left(first, first_send)

    @pl.when(gives_own & (y != z - 1))
    def _():
        left(own.at[0], own_send)

    @pl.when(on_chain & (z > y + 1))
    def _():
        left(u_out, u_send)

    @pl.when(solves)
    def _():
        for t in range(2, 4):

            @pl.when(t > z)
            def _(t=t):
                left(s_out, direct_send)

    @pl.when(solves | opens)
    def _():
        for t in range(8):
            left(s_out, plane_send)


def write(solved, remaining, solved_out, remaining_out):
    solved_out[...] = solved[...]
    remaining_out[...] = remaining[...]


def solution(mesh):
    def on_device(factor, rhs, inverses):
        steps = inverses.shape[0]
        blocks, width, nrhs = factor.shape[0], factor.shape[3], rhs.shape[4]
        chunks = len(CHUNKS)
        vmem, dma = pltpu.VMEM, pltpu.SemaphoreType.DMA
        shapes = (
            jax.ShapeDtypeStruct((steps, 16, nrhs), F32),
            jax.ShapeDtypeStruct((blocks, 128, nrhs), F32),
        )
        results = pl.pallas_call(
            kernel,
            out_shape=shapes,
            in_specs=[pl.BlockSpec(memory_space=pl.ANY)] * 3,
            out_specs=(pl.BlockSpec(memory_space=pltpu.VMEM),) * 2,
            scratch_shapes=[
                vmem((blocks, width, width), F32),
                vmem((blocks, width, width), BF16),
                vmem((blocks, width, width), BF16),
                vmem((2, width, width), F32),
                vmem((2, width, width), BF16),
                vmem((2, width, width), BF16),
                vmem((width, width), F32),
                vmem((width, width), BF16),
                vmem((width, width), BF16),
                vmem((blocks, 128, nrhs), F32),
                vmem((blocks, nrhs, 128), F32),
                vmem((4, 128, nrhs), F32),
                vmem((4, 128, nrhs), F32),
                vmem((nrhs, width), F32),
                vmem((nrhs, width), F32),
                vmem((nrhs, width), F32),
                vmem((2, nrhs, width), F32),
                vmem((nrhs, width), F32),
                vmem((nrhs, width), F32),
                vmem((nrhs, width), F32),
                vmem((4, blocks, nrhs, 128), F32),
                vmem((4, blocks, nrhs, 128), F32),
                vmem((4, 128, nrhs), F32),
                vmem((4, 16, nrhs), F32),
                dma((blocks,)),
                dma((2,)),
                dma,
                dma,
                dma,
                dma((4,)),
                dma,
                dma((4,)),
                dma,
                dma((chunks,)),
                dma,
                dma((2, chunks)),
                dma,
                dma,
                dma((chunks,)),
                dma,
                dma((4, chunks)),
                dma,
                dma((4,)),
            ],
            compiler_params=pltpu.CompilerParams(
                collective_id=0, has_side_effects=True, vmem_limit_bytes=56 * 2**20
            ),
        )(factor, rhs, inverses)
        solved, remaining = pl.pallas_call(
            write,
            out_shape=shapes,
            in_specs=[pl.BlockSpec(memory_space=pltpu.VMEM)] * 2,
            out_specs=(pl.BlockSpec(memory_space=pltpu.VMEM),) * 2,
        )(*results)
        return solved, remaining[:, None, None]

    return jax.shard_map(
        on_device,
        mesh=mesh,
        in_specs=(P(None, "row", "col", None, None), P(None, "row", "col", None, None), P()),
        out_specs=(P(None, "col", None), P(None, "row", "col", None, None)),
        check_vma=False,
    )
```

```python
import jax
import jax.numpy as jnp
from jax import lax
from jax.experimental import pallas as pl
from jax.experimental.pallas import tpu as pltpu
from jax.sharding import PartitionSpec as P

MESH = pl.DeviceIdType.MESH
F32 = jnp.float32
BF16 = jnp.bfloat16
SIZES = (24, 24, 24, 24, 16, 16)
CHUNKS = tuple((sum(SIZES[:q]), n) for q, n in enumerate(SIZES))


def split(x):
    hi = x.astype(BF16)
    return hi, (x - hi.astype(F32)).astype(BF16)


def product(x, hi, lo, transposed=False):
    dims = (((1,), (1 if transposed else 0,)), ((), ()))
    m = x.shape[0]
    x_hi, x_lo = split(x)
    both = lax.dot_general(
        jnp.concatenate([x_hi, x_lo], axis=0), hi, dims, preferred_element_type=F32
    )
    return both[:m] + (both[m:] + lax.dot_general(x_hi, lo, dims, preferred_element_type=F32))


def kernel(
    factor, rhs, inverses, solved_out, remaining_out,
    f32_buf, f_hi, f_lo, inv_f32, inv_hi, inv_lo, m_f32, m_hi, m_lo, rhs_buf, total,
    first, own, first_t, own_t, direct, u_in, u_out, s_out, gathered,
    parts, received, turned, solved_in,
    f_sem, inv_sem, rhs_sem, self_sem,
    first_send, first_recv, own_send, own_recv, direct_send, direct_recv, u_send, u_recv,
    plane_send, relay_send, plane_recv, part_send, part_recv, solved_send, solved_recv,
):
    row = lax.axis_index("row")
    col = lax.axis_index("col")
    y = col // 8
    z = lax.rem(col, 8)
    blocks = f_hi.shape[0]

    on_chain = (row == 0) & (y < z) & (z <= 3)
    starts = on_chain & (y == 0)
    solves = on_chain & (z == y + 1)
    opens = (row == 4) & (col == 0)
    gives_first = (row == 0) & (z == 0)
    gives_own = (row == 0) & (z >= 1) & (z <= 3)
    relay_row = jnp.where(y == 0, 5, 1)
    relays = row == relay_row

    def remote(src, dst, send, recv, to_row, to_col):
        return pltpu.make_async_remote_copy(
            src_ref=src, dst_ref=dst, send_sem=send, recv_sem=recv,
            device_id=(to_row, to_col), device_id_type=MESH,
        )

    def landed(ref, sem):
        remote(ref, ref, sem, sem, row, col).wait_recv()

    def left(ref, sem):
        remote(ref, ref, sem, sem, row, col).wait_send()

    def each(n, body):
        lax.fori_loop(0, n, lambda i, _: (body(i), 0)[1], 0)

    barrier = pltpu.get_barrier_semaphore()

    def greet(to_row, to_col):
        pl.semaphore_signal(barrier, inc=1, device_id=(to_row, to_col), device_id_type=MESH)

    @pl.when(starts | opens)
    def _():
        for p in range(4):
            greet(0, p * 8)

    for d in range(1, 4):
        greet(row, lax.rem(col + 8 * d, 32))

    @pl.when(relays)
    def _():
        greet(jnp.where(y == 0, 4, 0), jnp.where(y == 0, 0, (y - 1) * 8 + y))

    @pl.when(on_chain & (y > 0))
    def _():
        greet(0, (y - 1) * 8 + y)

    @pl.when(jnp.logical_not(relays))
    def _():
        greet(relay_row, col)

    def f_load(a):
        return pltpu.make_async_copy(factor.at[a, 0, 0], f32_buf.at[a], f_sem.at[a])

    def inv_load(k, slot):
        return pltpu.make_async_copy(inverses.at[k], inv_f32.at[slot], inv_sem.at[slot])

    @pl.when(starts | opens)
    def _():
        inv_load(0, 0).start()

    @pl.when(on_chain)
    def _():
        inv_load(z, 1).start()

    for a in range(blocks):
        f_load(a).start()
    rhs_load = pltpu.make_async_copy(rhs.at[:, 0, 0], rhs_buf, rhs_sem)
    rhs_load.start()
    self_load = pltpu.make_async_copy(rhs.at[0, 0, 0], own.at[y], self_sem)

    @pl.when(solves)
    def _():
        self_load.start()

    def split_inverse(k, slot):
        inv_load(k, slot).wait()
        hi, lo = split(inv_f32[slot])
        inv_hi[slot] = hi
        inv_lo[slot] = lo

    def split_factor(a):
        f_load(a).wait()
        hi, lo = split(f32_buf[a])
        f_hi[a] = hi
        f_lo[a] = lo

    @pl.when(starts | opens)
    def _():
        split_inverse(0, 0)

    split_factor(0)

    def fold(source):
        def some(b):
            rows = pl.ds(pl.multiple_of(b * 128, 128), 128)
            m_f32[rows] = source(rows)

        each(4, some)

    def split_m():
        hi, lo = split(m_f32[...])
        m_hi[...] = hi
        m_lo[...] = lo

    @pl.when(on_chain)
    def _():
        split_inverse(z, 1)
        fold(lambda rows: product(f32_buf[0, rows], inv_hi[1], inv_lo[1], True))
        split_m()

        @pl.when(y == 0)
        def _():
            for b in range(4):
                for c in range(4):
                    f32_buf[0, 128 * b : 128 * (b + 1), 128 * c : 128 * (c + 1)] = inv_f32[
                        0, 128 * c : 128 * (c + 1), 128 * b : 128 * (b + 1)
                    ].T
            fold(lambda rows: product(f32_buf[0, rows], m_hi[...], m_lo[...]))
            split_m()

    greeted = 3
    greeted += jnp.where(gives_first, 4, 0)
    greeted += jnp.where(solves | opens, 8, 0)
    greeted += jnp.where(solves & (z < 3), 3 - z, 0)
    greeted += jnp.where(relays, 7, 0)
    pl.semaphore_wait(barrier, greeted)

    @pl.when(gives_first)
    def _():
        for t in range(1, 4):
            remote(rhs.at[0, 0, 0], first.at[y], first_send, first_recv.at[y], 0, t).start()
        remote(rhs.at[0, 0, 0], first.at[y], first_send, first_recv.at[y], 4, 0).start()

    @pl.when(gives_own & (y != z - 1))
    def _():
        remote(rhs.at[0, 0, 0], own.at[y], own_send, own_recv.at[y], 0, (z - 1) * 8 + z).start()

    def prepare():
        lax.fori_loop(1, blocks, lambda a, _: (split_factor(a), 0)[1], 0)
        rhs_load.wait()

        def turn(a):
            total[a] = rhs_buf[a].T

        each(blocks, turn)

    early = starts | opens

    @pl.when(jnp.logical_not(early))
    def _():
        prepare()

    def rows_of(q):
        return pl.ds(*CHUNKS[q])

    def each_chunk(body):
        for q in range(len(CHUNKS)):
            body(q)

    def spread(q, plane):
        relay_to = jnp.where(opens, 5, 1)
        for d in (4, 3, 5, 2, 6, 1, 7, 0):
            remote(
                s_out.at[rows_of(q)], gathered.at[rows_of(q)], plane_send, plane_recv.at[q],
                relay_to, plane * 8 + lax.rem(z + d, 8),
            ).start()

    @pl.when(solves)
    def _():
        self_load.wait()
        for p in range(4):

            @pl.when(p != y)
            def _(p=p):
                landed(own.at[p], own_recv.at[p])

            own_t[:, 128 * p : 128 * (p + 1)] = own[p].T

        own_t[...] = product(own_t[...], inv_hi[1], inv_lo[1], True)

    @pl.when(early)
    def _():
        for p in (0, 1, 3, 2):
            landed(first.at[p], first_recv.at[p])
            first_t[:, 128 * p : 128 * (p + 1)] = first[p].T

    @pl.when(opens)
    def _():
        def open_chunk(q):
            s_out[rows_of(q)] = product(first_t[rows_of(q)], inv_hi[0], inv_lo[0], True)
            spread(q, 0)

        each_chunk(open_chunk)

    @pl.when(on_chain)
    def _():
        def chain_chunk(q):
            rows = rows_of(q)

            @pl.when(y == 0)
            def _():
                direct[rows] = first_t[rows]

            @pl.when(y > 0)
            def _():
                landed(direct.at[rows], direct_recv.at[q])

            u = product(direct[rows], m_hi[...], m_lo[...])

            @pl.when(z > y + 1)
            def _():
                u_out[rows] = u
                remote(
                    u_out.at[rows], u_in.at[y, rows], u_send, u_recv.at[y, q], 0, (z - 1) * 8 + z
                ).start()

            @pl.when(z == y + 1)
            def _():
                s_out[rows] = own_t[rows] - u
                for j in range(2):

                    @pl.when(j < y)
                    def _(j=j):
                        landed(u_in.at[j, rows], u_recv.at[j, q])
                        s_out[rows] = s_out[rows] - u_in[j, rows]

                for t in range(2, 4):

                    @pl.when(t > z)
                    def _(t=t):
                        remote(
                            s_out.at[rows], direct.at[rows], direct_send, direct_recv.at[q],
                            0, z * 8 + t,
                        ).start()

                @pl.when(z >= 2)
                def _():
                    spread(q, z)

        each_chunk(chain_chunk)

        @pl.when((y == 0) & (z == 1))
        def _():
            each_chunk(lambda q: spread(q, z))

    @pl.when(early)
    def _():
        prepare()

    keep = jnp.where((row == 0) & (z <= y), 0.0, 1.0).astype(F32)

    def plane_chunk(q):
        rows = rows_of(q)

        landed(gathered.at[rows], plane_recv.at[q])

        @pl.when(relays)
        def _():
            for d in (3, 5, 4, 6, 1, 2, 7):
                remote(
                    gathered.at[rows], gathered.at[rows], relay_send, plane_recv.at[q],
                    lax.rem(row + d, 8), col,
                ).start()

        s = gathered[rows]

        def one(a):
            u = product(s, f_hi[a], f_lo[a])
            u = jnp.where(a == 0, u * keep, u)
            for p in range(4):
                parts[p, a, rows] = u[:, 128 * p : 128 * (p + 1)]

            received[y, a, rows] = parts[y, a, rows]
            for i in range(3):
                to = lax.rem(y + 1 + lax.rem(i + 1 - lax.rem(y, 2), 3), 4)
                remote(
                    parts.at[to, a, rows], received.at[y, a, rows], part_send, part_recv.at[y, q],
                    row, to * 8 + z,
                ).start()

        each(blocks, one)

    each_chunk(plane_chunk)

    for b in range(4):
        turned[b] = gathered[:, 128 * b : 128 * (b + 1)].T
    rows = pl.ds(pl.multiple_of(z * 16, 16), 16)
    for d in range(1, 4):
        to = lax.rem(y + d, 4)
        remote(
            turned.at[to, rows], solved_in.at[y], solved_send, solved_recv.at[y], row, to * 8 + z
        ).start()
    solved_in[y] = turned[y, rows]

    for k in range(4):

        def reduce(q, k=k):
            @pl.when(k != y)
            def _():
                landed(received.at[k, :, rows_of(q)], part_recv.at[k, q])

            def one(a):
                total[a, rows_of(q)] = total[a, rows_of(q)] - received[k, a, rows_of(q)]

            each(blocks, one)

        each_chunk(reduce)

    for a in range(blocks):
        remaining_out[a] = total[a].T
    for k in range(4):

        @pl.when(k != y)
        def _(k=k):
            landed(solved_in.at[k], solved_recv.at[k])

    solved_out[...] = solved_in[...]

    left(solved_in.at[pl.ds(0, 3)], solved_send)
    left(received.at[pl.ds(0, 3)], part_send)

    @pl.when(relays)
    def _():
        for t in range(1, 8):
            left(gathered, relay_send)

    @pl.when(gives_first)
    def _():
        left(first, first_send)

    @pl.when(gives_own & (y != z - 1))
    def _():
        left(own.at[0], own_send)

    @pl.when(on_chain & (z > y + 1))
    def _():
        left(u_out, u_send)

    @pl.when(solves)
    def _():
        for t in range(2, 4):

            @pl.when(t > z)
            def _(t=t):
                left(s_out, direct_send)

    @pl.when(solves | opens)
    def _():
        for t in range(8):
            left(s_out, plane_send)


def solution(mesh):
    def on_device(factor, rhs, inverses):
        steps = inverses.shape[0]
        blocks, width, nrhs = factor.shape[0], factor.shape[3], rhs.shape[4]
        chunks = len(CHUNKS)
        vmem, dma = pltpu.VMEM, pltpu.SemaphoreType.DMA
        shapes = (
            jax.ShapeDtypeStruct((steps, 16, nrhs), F32),
            jax.ShapeDtypeStruct((blocks, 128, nrhs), F32),
        )
        solved, remaining = pl.pallas_call(
            kernel,
            out_shape=tuple(vmem(t.shape, t.dtype) for t in shapes),
            in_specs=[pl.BlockSpec(memory_space=pl.ANY)] * 3,
            out_specs=(pl.BlockSpec(memory_space=pltpu.VMEM),) * 2,
            scratch_shapes=[
                vmem((blocks, width, width), F32),
                vmem((blocks, width, width), BF16),
                vmem((blocks, width, width), BF16),
                vmem((2, width, width), F32),
                vmem((2, width, width), BF16),
                vmem((2, width, width), BF16),
                vmem((width, width), F32),
                vmem((width, width), BF16),
                vmem((width, width), BF16),
                vmem((blocks, 128, nrhs), F32),
                vmem((blocks, nrhs, 128), F32),
                vmem((4, 128, nrhs), F32),
                vmem((4, 128, nrhs), F32),
                vmem((nrhs, width), F32),
                vmem((nrhs, width), F32),
                vmem((nrhs, width), F32),
                vmem((2, nrhs, width), F32),
                vmem((nrhs, width), F32),
                vmem((nrhs, width), F32),
                vmem((nrhs, width), F32),
                vmem((4, blocks, nrhs, 128), F32),
                vmem((4, blocks, nrhs, 128), F32),
                vmem((4, 128, nrhs), F32),
                vmem((4, 16, nrhs), F32),
                dma((blocks,)),
                dma((2,)),
                dma,
                dma,
                dma,
                dma((4,)),
                dma,
                dma((4,)),
                dma,
                dma((chunks,)),
                dma,
                dma((2, chunks)),
                dma,
                dma,
                dma((chunks,)),
                dma,
                dma((4, chunks)),
                dma,
                dma((4,)),
            ],
            compiler_params=pltpu.CompilerParams(
                collective_id=0, has_side_effects=True, vmem_limit_bytes=56 * 2**20
            ),
        )(factor, rhs, inverses)
        return solved, remaining[:, None, None]

    return jax.shard_map(
        on_device,
        mesh=mesh,
        in_specs=(P(None, "row", "col", None, None), P(None, "row", "col", None, None), P()),
        out_specs=(P(None, "col", None), P(None, "row", "col", None, None)),
        check_vma=False,
    )
```
